512 devices in a mesh: dp: 32 (over z, core), tensor: 16 (over y, x).
Axes of the slice: x: 4, y: 4, z: 16, core: 2. Of those that a mesh axis runs over, the one named last changes fastest.
Arguments:
- dout: bfloat16 [12288, 5120], P(('dp', 'tensor')), may hold values from -0.75 to 0.75
- attn_ctx: bfloat16 [12288, 5120], P('dp', 'tensor'), may hold values from -6 to 6
- mlp_hidden: bfloat16 [12288, 13824], P('dp', 'tensor'), may hold values from -6 to 6
- w_out: bfloat16 [5120, 5120], P('tensor', 'dp'), may hold values from -0.078125 to 0.078125
- w_down: bfloat16 [13824, 5120], P('tensor', 'dp'), may hold values from -0.0546875 to 0.0546875
- head_logits: float32 [40], replicated, may hold values from -2 to 3
- unit_logits: float32 [13824], P('tensor'), may hold values from -2 to 3
- head_noise: float32 [40], replicated, may hold values from 0.001 to 0.999
- unit_noise: float32 [13824], P('tensor'), may hold values from 0.001 to 0.999
- linear_mult: float32 [1], replicated, may hold values from 100 to 300
- square_mult: float32 [1], replicated, may hold values from 1 to 4
- target: float32 [1], replicated, may hold values from 40 to 70
Outputs:
- ctx_grad: bfloat16 [12288, 5120], P('dp', 'tensor')
- hidden_grad: bfloat16 [12288, 13824], P('dp', 'tensor')
- head_grad: float32 [40], replicated
- unit_grad: float32 [13824], P('tensor')
The draws below stay inside these ranges and needn't reach their ends.
All inputs are finite; a program needn't handle non-finite values.
Results may differ from the reference program's by a relative error of at most 0.001.
Values may be sent and summed in bfloat16 or wider, within the bound.
No kernel may reach another device: no remote copies, remote signals or barrier semaphores. Data moves between devices by JAX's collectives and lax.ppermute only.
A program may use at most 64 MiB of HBM per device.

```python
import jax
import jax.numpy as jnp
from jax import lax

D = 5120
H = 40
HEAD = 128
FF = 13824
TOK = 384
HD = 5120
TOKENS = 12288


def block_scale(rng, shape, cuts, least, high):
    def one(dim, shards_of):
        heights = jax.random.uniform(jax.random.fold_in(jax.random.fold_in(rng, 6), dim), (shards_of,), jnp.float32, least / len(cuts), high / len(cuts))
        return jnp.repeat(jnp.exp(heights), shape[dim] // shards_of).reshape((-1,) + (1,) * (len(shape) - dim - 1))

    loudness = one(*cuts[0])
    for cut in cuts[1:]:
        loudness = loudness * one(*cut)
    return loudness


def scatter_about(stream_key, shape, spread, limit, cuts=(), kind=jnp.bfloat16):
    entries = jax.random.normal(stream_key, shape, jnp.float32) * spread
    if len(cuts) > 0:
        entries = block_scale(stream_key, shape, cuts, -0.22, 0.18) * entries
    return jnp.clip(entries, min=-limit, max=limit).astype(kind)


def setup_inputs(seed: int = 0) -> dict:
    arg_keys = jax.random.split(jax.random.key(seed), 13)
    dout = scatter_about(arg_keys[0], (TOKENS, D), 0.125, 0.75, ((0, 512),))
    attn_ctx = scatter_about(arg_keys[1], (TOKENS, HD), 1.0, 6.0, ((0, 32), (1, 16)))
    mlp_hidden = scatter_about(arg_keys[2], (TOKENS, FF), 1.0, 6.0, ((0, 32), (1, 16)))
    w_out = scatter_about(arg_keys[3], (HD, D), HD ** -0.5, 0.078125, ((0, 16), (1, 32)))
    w_down = scatter_about(arg_keys[4], (FF, D), FF ** -0.5, 0.0546875, ((0, 16), (1, 32)))
    head_logits = jnp.clip(jax.random.uniform(arg_keys[5], (H,), jnp.float32, -2.0, 3.0), -2.0, 3.0)
    unit_logits = jnp.clip(-2.0 + 5.0 * jax.random.uniform(arg_keys[6], (FF,), jnp.float32) ** block_scale(arg_keys[6], (FF,), ((0, 16),), -0.2, 0.2), -2.0, 3.0)
    head_noise = jnp.clip(jax.random.uniform(arg_keys[7], (H,), jnp.float32, 0.001, 0.999), 0.001, 0.999)
    unit_noise = jnp.clip(0.001 + 0.998 * jax.random.uniform(arg_keys[8], (FF,), jnp.float32) ** block_scale(arg_keys[8], (FF,), ((0, 16),), -0.2, 0.2), 0.001, 0.999)
    linear_mult = jnp.clip(jax.random.uniform(arg_keys[9], (1,), jnp.float32, 100.0, 300.0), 100.0, 300.0)
    square_mult = jnp.clip(jax.random.uniform(arg_keys[10], (1,), jnp.float32, 1.0, 4.0), 1.0, 4.0)
    target = jnp.clip(jax.random.uniform(arg_keys[11], (1,), jnp.float32, 40.0, 70.0), 40.0, 70.0)
    return {"dout": dout, "attn_ctx": attn_ctx, "mlp_hidden": mlp_hidden, "w_out": w_out, "w_down": w_down, "head_logits": head_logits, "unit_logits": unit_logits, "head_noise": head_noise, "unit_noise": unit_noise, "linear_mult": linear_mult, "square_mult": square_mult, "target": target}


low_end = -0.1
high_end = 1.1
temper = 2.0 / 3.0


def concrete(logits, noise):
    shape_s = jax.nn.sigmoid((jnp.log(noise) - jnp.log(1.0 - noise) + logits) / temper)
    stretched = shape_s * (high_end - low_end) + low_end
    gate = jnp.clip(stretched, 0.0, 1.0)
    inside = jnp.logical_and(stretched > 0.0, stretched < 1.0)
    slope = jnp.where(inside, (high_end - low_end) / temper * shape_s * (1.0 - shape_s), 0.0 * shape_s)
    return gate, slope


def open_prob(logits):
    return jax.nn.sigmoid(logits - temper * jnp.log(-low_end / high_end))


def reference(dout, attn_ctx, mlp_hidden, w_out, w_down, head_logits, unit_logits, head_noise, unit_noise, linear_mult, square_mult, target):
    head_gate, head_slope = concrete(head_logits, head_noise)
    unit_gate, unit_slope = concrete(unit_logits, unit_noise)
    col_gate = jnp.repeat(head_gate, HEAD)
    blocks = TOKENS // TOK
    dy_blocks = dout.reshape(blocks, TOK, D)
    ctx_blocks = attn_ctx.reshape(blocks, TOK, H * HEAD)
    hid_blocks = mlp_hidden.reshape(blocks, TOK, FF)
    dims = (((1,), (1,)), ((), ()))

    def step(carry, pieces):
        dy_block, ctx_block, hid_block = pieces
        ctx_pre = lax.dot_general(dy_block, w_out, dims, preferred_element_type=jnp.float32)
        hid_pre = lax.dot_general(dy_block, w_down, dims, preferred_element_type=jnp.float32)
        ctx_out = (ctx_pre * col_gate[None, :]).astype(jnp.bfloat16)
        hid_out = (hid_pre * unit_gate[None, :]).astype(jnp.bfloat16)
        col_acc = carry[0] + jnp.sum(ctx_block.astype(jnp.float32) * ctx_pre, axis=0)
        unit_acc = carry[1] + jnp.sum(hid_block.astype(jnp.float32) * hid_pre, axis=0)
        return (col_acc, unit_acc), (ctx_out, hid_out)

    start = (jnp.zeros((H * HEAD,), jnp.float32), jnp.zeros((FF,), jnp.float32))
    (col_data, unit_data), (ctx_out, hid_out) = lax.scan(step, start, (dy_blocks, ctx_blocks, hid_blocks))
    head_data = jnp.sum(col_data.reshape(H, HEAD), axis=1)
    p_head = open_prob(head_logits)
    p_unit = open_prob(unit_logits)
    denom = 4.0 * HEAD * H + 3.0 * FF
    size = 100.0 * (4.0 * HEAD * jnp.sum(p_head) + 3.0 * jnp.sum(p_unit)) / denom
    factor = linear_mult[0] + 2.0 * square_mult[0] * (size - target[0])
    head_grad = head_data * head_slope + factor * (400.0 * HEAD / denom) * p_head * (1.0 - p_head)
    unit_grad = unit_data * unit_slope + factor * (300.0 / denom) * p_unit * (1.0 - p_unit)
    ctx_grad = ctx_out.reshape(TOKENS, H * HEAD)
    hidden_grad = hid_out.reshape(TOKENS, FF)
    return ctx_grad, hidden_grad, head_grad, unit_grad
```

```python
import jax
import jax.numpy as jnp
from jax import lax
from jax.experimental import pallas as pl
from jax.experimental.pallas import tpu as pltpu
from jax.sharding import PartitionSpec as P

HEAD = 128
LANE = 128
TILE = 256

low_end = -0.1
high_end = 1.1
temper = 2.0 / 3.0


def concrete(logits, noise):
    shape_s = jax.nn.sigmoid((jnp.log(noise) - jnp.log(1.0 - noise) + logits) / temper)
    stretched = shape_s * (high_end - low_end) + low_end
    gate = jnp.clip(stretched, 0.0, 1.0)
    inside = jnp.logical_and(stretched > 0.0, stretched < 1.0)
    slope = jnp.where(
        inside, (high_end - low_end) / temper * shape_s * (1.0 - shape_s), 0.0 * shape_s
    )
    return (gate, slope)


def open_prob(logits):
    return jax.nn.sigmoid(logits - temper * jnp.log(-low_end / high_end))


def up(n, m):
    return -(-n // m) * m


def pad_to(x, n):
    return jnp.pad(x, ((0, 0), (0, n - x.shape[1])))


def pre_grads(rows, weight, act, gate, n_ctx, n_hid, copies):
    tokens, cols = act.shape
    depth = weight.shape[0]
    parts = len(rows)
    step_k = depth // parts
    hid_at = up(n_ctx, LANE)
    steps = cols // TILE

    def kernel(*refs):
        row_refs = refs[:parts]
        w_ref, act_ref, gate_ref, ctx_ref, hid_ref, sum_ref = refs[parts:]
        pre = jnp.zeros((tokens, TILE), jnp.float32)
        for q in range(parts):
            pre += jnp.dot(
                row_refs[q][...],
                w_ref[pl.ds(q * step_k, step_k), :],
                preferred_element_type=jnp.float32,
            )
        sums = jnp.sum(act_ref[...].astype(jnp.float32) * pre, axis=0, keepdims=True)
        sum_ref[...] = jnp.broadcast_to(sums, (copies, TILE))
        out = (pre * gate_ref[...]).astype(jnp.bfloat16).T
        j = pl.program_id(0)
        for s in range(steps):
            at = s * TILE

            @pl.when(j == s)
            def _():
                lo, hi = at, min(at + TILE, n_ctx)
                if hi > lo:
                    ctx_ref[pl.ds(lo, hi - lo), :] = out[lo - at : hi - at]
                lo, hi = max(at, hid_at), min(at + TILE, hid_at + n_hid)
                if hi > lo:
                    hid_ref[pl.ds(lo - hid_at, hi - lo), :] = out[lo - at : hi - at]

    whole = lambda shape: pl.BlockSpec(shape, lambda j: (0, 0))
    return pl.pallas_call(
        kernel,
        grid=(steps,),
        in_specs=[whole(r.shape) for r in rows]
        + [
            pl.BlockSpec((depth, TILE), lambda j: (0, j)),
            pl.BlockSpec((tokens, TILE), lambda j: (0, j)),
            pl.BlockSpec((1, TILE), lambda j: (0, j)),
        ],
        out_specs=[
            whole((n_ctx, tokens)),
            whole((n_hid, tokens)),
            pl.BlockSpec((copies, TILE), lambda j: (0, j)),
        ],
        out_shape=[
            jax.ShapeDtypeStruct((n_ctx, tokens), jnp.bfloat16),
            jax.ShapeDtypeStruct((n_hid, tokens), jnp.bfloat16),
            jax.ShapeDtypeStruct((copies, cols), jnp.float32),
        ],
        compiler_params=pltpu.CompilerParams(
            dimension_semantics=("arbitrary",), vmem_limit_bytes=56 * 2**20
        ),
        name="pre_grads",
    )(*rows, weight, act, gate)


def make_local(dp, tensor):
    side = 4
    along_x = [[b * side + i for i in range(side)] for b in range(tensor // side)]
    along_y = [[b + side * i for i in range(tensor // side)] for b in range(side)]

    def local(
        dout,
        attn_ctx,
        mlp_hidden,
        w_out,
        w_down,
        head_logits,
        unit_logits,
        head_noise,
        unit_noise,
        linear_mult,
        square_mult,
        target,
    ):
        n_ctx = attn_ctx.shape[1]
        n_hid = mlp_hidden.shape[1]
        p_ctx, p_hid = up(n_ctx, LANE), up(n_hid, LANE)
        heads = head_logits.shape[0]

        packed = jnp.concatenate([pad_to(w_out.T, p_ctx), pad_to(w_down.T, p_hid)], axis=1)
        weight = lax.all_gather(packed, "dp", axis=0, tiled=True)

        wide = lax.all_gather(dout, "tensor", axis=0, tiled=True, axis_index_groups=along_x)
        chunk = wide.shape[1] // 4
        rows = [
            lax.all_gather(
                wide[:, q * chunk : (q + 1) * chunk],
                "tensor",
                axis=0,
                tiled=True,
                axis_index_groups=along_y,
            )
            for q in range(4)
        ]

        head_gate, head_slope = concrete(head_logits, head_noise)
        unit_gate, unit_slope = concrete(unit_logits, unit_noise)
        tensor_index = lax.axis_index("tensor")
        columns = tensor_index * n_ctx + lax.iota(jnp.int32, n_ctx)
        owner = columns // HEAD
        member = (owner[:, None] == lax.iota(jnp.int32, heads)[None, :]).astype(jnp.float32)
        col_gate = jnp.dot(member, head_gate, precision=lax.Precision.HIGHEST)
        gate = jnp.concatenate(
            [pad_to(col_gate[None, :], p_ctx), pad_to(unit_gate[None, :], p_hid)], axis=1
        )
        act = jnp.concatenate([pad_to(attn_ctx, p_ctx), pad_to(mlp_hidden, p_hid)], axis=1)

        ctx_t, hid_t, sums = pre_grads(rows, weight, act, gate, n_ctx, n_hid, dp)

        data = jnp.sum(lax.all_to_all(sums, "dp", 0, 0, tiled=True), axis=0)
        unit_data = data[p_ctx : p_ctx + n_hid]
        head_part = jnp.dot(data[:n_ctx], member, precision=lax.Precision.HIGHEST)
        p_head = open_prob(head_logits)
        p_unit = open_prob(unit_logits)
        local_mass = jnp.sum(p_unit)
        mine = jnp.concatenate(
            [head_part, local_mass[None], jnp.zeros((LANE - heads - 1,), jnp.float32)]
        )
        both = jnp.sum(
            lax.all_to_all(jnp.broadcast_to(mine, (tensor, LANE)), "tensor", 0, 0, tiled=True),
            axis=0,
        )
        head_data, unit_mass = both[:heads], both[heads]

        denom = 4.0 * HEAD * heads + 3.0 * n_hid * tensor
        size = 100.0 * (4.0 * HEAD * jnp.sum(p_head) + 3.0 * unit_mass) / denom
        factor = linear_mult[0] + 2.0 * square_mult[0] * (size - target[0])
        head_grad = head_data * head_slope + factor * (400.0 * HEAD / denom) * p_head * (
            1.0 - p_head
        )
        unit_grad = unit_data * unit_slope + factor * (300.0 / denom) * p_unit * (1.0 - p_unit)
        return (ctx_t.T, hid_t.T, head_grad, unit_grad)

    return local


def solution(mesh):
    placed = (
        P(("dp", "tensor"), None),
        P("dp", "tensor"),
        P("dp", "tensor"),
        P("tensor", "dp"),
        P("tensor", "dp"),
        P(),
        P("tensor"),
        P(),
        P("tensor"),
        P(),
        P(),
        P(),
    )
    return jax.shard_map(
        make_local(mesh.shape["dp"], mesh.shape["tensor"]),
        mesh=mesh,
        in_specs=placed,
        out_specs=(P("dp", "tensor"), P("dp", "tensor"), P(), P("tensor")),
        check_vma=False,
    )
```

```python
import jax
import jax.numpy as jnp
from jax import lax
from jax.experimental import pallas as pl
from jax.experimental.pallas import tpu as pltpu
from jax.sharding import PartitionSpec as P

HEAD = 128
LANE = 128
TILE = 256

low_end = -0.1
high_end = 1.1
temper = 2.0 / 3.0


def concrete(logits, noise):
    shape_s = jax.nn.sigmoid((jnp.log(noise) - jnp.log(1.0 - noise) + logits) / temper)
    stretched = shape_s * (high_end - low_end) + low_end
    gate = jnp.clip(stretched, 0.0, 1.0)
    inside = jnp.logical_and(stretched > 0.0, stretched < 1.0)
    slope = jnp.where(
        inside, (high_end - low_end) / temper * shape_s * (1.0 - shape_s), 0.0 * shape_s
    )
    return (gate, slope)


def open_prob(logits):
    return jax.nn.sigmoid(logits - temper * jnp.log(-low_end / high_end))


def up(n, m):
    return -(-n // m) * m


def pad_to(x, n):
    return jnp.pad(x, ((0, 0), (0, n - x.shape[1])))


def column_sums(act, pre):
    return jnp.sum(act.astype(jnp.float32) * pre, axis=0, keepdims=True)


def fetch(weight, held, sems, first, count, parts):
    per = weight.shape[0] // parts
    copies = [
        [
            pltpu.make_async_copy(
                weight.at[pl.ds(q * per, per), first + j],
                held.at[j, pl.ds(q * per, per)],
                sems.at[j, q],
            )
            for q in range(parts)
        ]
        for j in range(count)
    ]
    for tile in copies:
        for c in tile:
            c.start()
    return copies


def product(rows, held, copies, j):
    shards, depth = held.shape[1], held.shape[2]
    per = shards // len(rows)
    pre = None
    for q, r in enumerate(rows):
        copies[j][q].wait()
        block = held[j, pl.ds(q * per, per)].reshape(per * depth, TILE)
        term = jnp.dot(r[...], block, preferred_element_type=jnp.float32)
        pre = term if pre is None else pre + term
    return pre


def gated(pre, gate):
    return (pre * gate).astype(jnp.bfloat16).T


def specs(n):
    return [pl.BlockSpec(memory_space=pltpu.VMEM) for _ in range(n)]


def held_scratch(weight, count, parts):
    return [
        pltpu.VMEM((count, weight.shape[0], weight.shape[2], TILE), weight.dtype),
        pltpu.SemaphoreType.DMA((count, parts)),
    ]


def context_part(rows, weight, act, gate, member, extra, n_ctx, n_hid, peers):
    tokens, cols = act.shape
    parts, count = len(rows), cols // TILE
    edge = up(n_ctx, LANE)
    rest = cols - edge

    def kernel(*refs):
        row_refs = refs[:parts]
        w, act_ref, gate_ref, member_ref, extra_ref = refs[parts : parts + 5]
        ctx_ref, hid_ref, sum_ref, head_ref, held, sems, out_buf, out_sem = refs[parts + 5 :]
        sent = pltpu.make_async_copy(out_buf, hid_ref.at[pl.ds(0, rest)], out_sem)
        copies = fetch(w, held, sems, 0, count, parts)
        sums = []
        for j in range(count):
            at = j * TILE
            pre = product(row_refs, held, copies, j)
            sums.append(column_sums(act_ref[:, pl.ds(at, TILE)], pre))
            out = gated(pre, gate_ref[:, pl.ds(at, TILE)])
            stop = min(at + TILE, n_ctx)
            ctx_ref[pl.ds(at, stop - at), :] = out[: stop - at]
            if at + TILE > edge:
                out_buf[...] = out[edge - at :]
                sent.start()
        line = jnp.concatenate(sums, axis=1)
        sum_ref[...] = line[:, edge:]
        part = jnp.dot(
            jnp.broadcast_to(line[:, :edge], (8, edge)),
            member_ref[...],
            precision=lax.Precision.HIGHEST,
            preferred_element_type=jnp.float32,
        )
        head_ref[...] = jnp.broadcast_to((part[:1] + extra_ref[...])[None], (peers, 1, LANE))
        sent.wait()

    return pl.pallas_call(
        kernel,
        in_specs=specs(parts) + [pl.BlockSpec(memory_space=pltpu.HBM)] + specs(4),
        out_specs=[
            pl.BlockSpec(),
            pl.BlockSpec(memory_space=pltpu.HBM),
            pl.BlockSpec(),
            pl.BlockSpec(),
        ],
        out_shape=[
            jax.ShapeDtypeStruct((n_ctx, tokens), jnp.bfloat16),
            jax.ShapeDtypeStruct((n_hid, tokens), jnp.bfloat16),
            jax.ShapeDtypeStruct((1, rest), jnp.float32),
            jax.ShapeDtypeStruct((peers, 1, LANE), jnp.float32),
        ],
        scratch_shapes=held_scratch(weight, count, parts)
        + [pltpu.VMEM((rest, tokens), jnp.bfloat16), pltpu.SemaphoreType.DMA],
        compiler_params=pltpu.CompilerParams(vmem_limit_bytes=12 * 2**20),
        name="context_part",
    )(*rows, weight, act, gate, member, extra)


def hidden_part(rows, weight, first, act, gate, begun, done):
    tokens, cols = act.shape
    parts, count = len(rows), cols // TILE
    n_hid = begun.shape[0]

    def kernel(*refs):
        row_refs = refs[:parts]
        w, act_ref, gate_ref, _, hid_ref, sum_ref, held, sems, out_buf, out_sems = refs[parts:]
        copies = fetch(w, held, sems, first, count, parts)
        sent = []
        for j in range(count):
            at = j * TILE
            pre = product(row_refs, held, copies, j)
            out = gated(pre, gate_ref[:, pl.ds(at, TILE)])
            size = min(TILE, n_hid - done - at)
            out_buf[j] = out
            sent.append(
                pltpu.make_async_copy(
                    out_buf.at[j, pl.ds(0, size)],
                    hid_ref.at[pl.ds(done + at, size)],
                    out_sems.at[j],
                )
            )
            sent[j].start()
            sum_ref[:, pl.ds(at, TILE)] = column_sums(act_ref[:, pl.ds(at, TILE)], pre)
        for c in sent:
            c.wait()

    return pl.pallas_call(
        kernel,
        in_specs=specs(parts)
        + [pl.BlockSpec(memory_space=pltpu.HBM)]
        + specs(2)
        + [pl.BlockSpec(memory_space=pltpu.HBM)],
        out_specs=[pl.BlockSpec(memory_space=pltpu.HBM), pl.BlockSpec()],
        out_shape=[
            jax.ShapeDtypeStruct((n_hid, tokens), jnp.bfloat16),
            jax.ShapeDtypeStruct((1, cols), jnp.float32),
        ],
        scratch_shapes=held_scratch(weight, count, parts)
        + [pltpu.VMEM((count, TILE, tokens), jnp.bfloat16), pltpu.SemaphoreType.DMA((count,))],
        input_output_aliases={parts + 3: 0},
        compiler_params=pltpu.CompilerParams(vmem_limit_bytes=16 * 2**20),
        name="hidden_part",
    )(*rows, weight, act, gate, begun)


def pack(w_ctx, w_hid, p_ctx, p_hid):
    depth, n_ctx = w_ctx.shape
    n_hid = w_hid.shape[1]

    def kernel(ctx_ref, hid_ref, out_ref):
        for at in range(0, p_ctx + p_hid, LANE):
            rows = pl.ds(at // TILE * depth, depth)
            src, lo, n = (ctx_ref, at, n_ctx) if at < p_ctx else (hid_ref, at - p_ctx, n_hid)
            size = min(LANE, n - lo)
            out_ref[rows, pl.ds(at % TILE, size)] = src[:, pl.ds(lo, size)]
            if size < LANE:
                out_ref[rows, pl.ds(at % TILE + size, LANE - size)] = jnp.zeros(
                    (depth, LANE - size), out_ref.dtype
                )

    return pl.pallas_call(
        kernel,
        out_shape=jax.ShapeDtypeStruct(((p_ctx + p_hid) // TILE * depth, TILE), w_ctx.dtype),
        compiler_params=pltpu.CompilerParams(vmem_limit_bytes=4 * 2**20),
        name="pack",
    )(w_ctx, w_hid)


def line_up(heads, first, second, copies):
    a, b = first.shape[1], second.shape[1]

    def kernel(heads_ref, first_ref, second_ref, out_ref):
        total = jnp.sum(heads_ref[...], axis=0)
        line = jnp.concatenate([first_ref[...], second_ref[...], total], axis=1)
        out_ref[...] = jnp.broadcast_to(line[None], (copies, 1, a + b + LANE))

    return pl.pallas_call(
        kernel,
        out_shape=jax.ShapeDtypeStruct((copies, 1, a + b + LANE), jnp.float32),
        compiler_params=pltpu.CompilerParams(vmem_limit_bytes=4 * 2**20),
        name="line_up",
    )(heads, first, second)


def make_local(dp, tensor):
    side = 4
    along_x = [[b * side + i for i in range(side)] for b in range(tensor // side)]
    along_y = [[b + side * i for i in range(tensor // side)] for b in range(side)]

    def local(
        dout,
        attn_ctx,
        mlp_hidden,
        w_out,
        w_down,
        head_logits,
        unit_logits,
        head_noise,
        unit_noise,
        linear_mult,
        square_mult,
        target,
    ):
        n_ctx = attn_ctx.shape[1]
        n_hid = mlp_hidden.shape[1]
        p_ctx, p_hid = up(n_ctx, LANE), up(n_hid, LANE)
        heads = head_logits.shape[0]

        packed = pack(w_out.T, w_down.T, p_ctx, p_hid)
        tiles = (p_ctx + p_hid) // TILE
        weight = lax.all_gather(packed, "dp", axis=0, tiled=True)
        weight = weight.reshape(dp, tiles, w_out.shape[1], TILE)
        weight = pltpu.with_memory_space_constraint(weight, pltpu.HBM)

        wide = lax.all_gather(dout, "tensor", axis=0, tiled=True, axis_index_groups=along_x)
        chunk = wide.shape[1] // 4
        rows = [
            lax.all_gather(
                wide[:, q * chunk : (q + 1) * chunk],
                "tensor",
                axis=0,
                tiled=True,
                axis_index_groups=along_y,
            )
            for q in range(4)
        ]

        head_gate, head_slope = concrete(head_logits, head_noise)
        unit_gate, unit_slope = concrete(unit_logits, unit_noise)
        tensor_index = lax.axis_index("tensor")
        columns = tensor_index * n_ctx + lax.iota(jnp.int32, n_ctx)
        owner = columns // HEAD
        member = (owner[:, None] == lax.iota(jnp.int32, heads)[None, :]).astype(jnp.float32)
        col_gate = jnp.dot(member, head_gate, precision=lax.Precision.HIGHEST)
        p_head = open_prob(head_logits)
        p_unit = open_prob(unit_logits)
        gate = jnp.concatenate(
            [pad_to(col_gate[None, :], p_ctx), pad_to(unit_gate[None, :], p_hid)], axis=1
        )
        act = jnp.concatenate([pad_to(attn_ctx, p_ctx), pad_to(mlp_hidden, p_hid)], axis=1)
        cut = up(p_ctx, TILE)
        member = jnp.pad(member, ((0, p_ctx - n_ctx), (0, LANE - heads)))
        extra = jnp.where(
            lax.broadcasted_iota(jnp.int32, (1, LANE), 1) == heads, jnp.sum(p_unit), 0.0
        )

        ctx_t, begun, first_sums, head_rows = context_part(
            rows, weight, act[:, :cut], gate[:, :cut], member, extra, n_ctx, n_hid, tensor
        )
        head_rows = lax.all_to_all(head_rows, "tensor", 0, 0, tiled=True)
        hid_t, second_sums = hidden_part(
            rows, weight, cut // TILE, act[:, cut:], gate[:, cut:], begun, cut - p_ctx
        )
        lines = line_up(head_rows, first_sums, second_sums, dp)
        data = jnp.sum(lax.all_to_all(lines, "dp", 0, 0, tiled=True), axis=(0, 1))
        unit_data = data[:n_hid]
        head_data = data[p_hid : p_hid + heads]
        unit_mass = data[p_hid + heads] / dp

        denom = 4.0 * HEAD * heads + 3.0 * n_hid * tensor
        size = 100.0 * (4.0 * HEAD * jnp.sum(p_head) + 3.0 * unit_mass) / denom
        factor = linear_mult[0] + 2.0 * square_mult[0] * (size - target[0])
        head_grad = head_data * head_slope + factor * (400.0 * HEAD / denom) * p_head * (
            1.0 - p_head
        )
        unit_grad = unit_data * unit_slope + factor * (300.0 / denom) * p_unit * (1.0 - p_unit)
        return (ctx_t.T, hid_t.T, head_grad, unit_grad)

    return local


def solution(mesh):
    placed = (
        P(("dp", "tensor"), None),
        P("dp", "tensor"),
        P("dp", "tensor"),
        P("tensor", "dp"),
        P("tensor", "dp"),
        P(),
        P("tensor"),
        P(),
        P("tensor"),
        P(),
        P(),
        P(),
    )
    return jax.shard_map(
        make_local(mesh.shape["dp"], mesh.shape["tensor"]),
        mesh=mesh,
        in_specs=placed,
        out_specs=(P("dp", "tensor"), P("dp", "tensor"), P(), P("tensor")),
        check_vma=False,
    )
```
